32 devices in a mesh: client: 4 (over x, core), blk: 8 (over z, y).
Axes of the slice: x: 2, y: 2, z: 4, core: 2. Of those that a mesh axis runs over, the one named last changes fastest.
Arguments:
- activations: bfloat16 [8, 2, 8, 8, 1280], P('client', None, 'blk'), may hold values from -6 to 6
- sample_count: int32 [8], replicated, may hold values from 1 to 2, as said below
- client_weights: bfloat16 [8, 11520, 1280], P('client', 'blk'), may hold values from -6 to 6
Outputs:
- merged_gram: float32 [11520, 11520], P(('blk', 'client'))
- merged_rhs: float32 [11520, 1280], P(('blk', 'client'))
The draws below stay inside these ranges and needn't reach their ends.
Inputs may be any that keep to these rules, and one draw needn't show every extreme that they name: `sample_count`: some client has all 2 slots live in every draw.
All inputs are finite; a program needn't handle non-finite values.
Results may differ from the reference program's by a relative error of at most 0.0029.
Values may be sent and summed in bfloat16 or wider, within the bound.
A program may use at most 192 MiB of HBM per device.

```python
import jax
import jax.numpy as jnp
from jax import lax

CH = 1280
COUT = 1280
IMG_W = 8
SLOTS = 2
CLIENTS = 8
HH = 8
KK = 11520


def draw_sample_count(key, part):
    first_key, second_key = jax.random.split(jax.random.fold_in(key, 17))
    counts_drawn = jax.random.randint(first_key, (CLIENTS,), 1, SLOTS + 1)
    filled_client = jax.random.randint(second_key, (), 0, CLIENTS)
    positions = jnp.arange(CLIENTS)
    return jnp.where(positions == filled_client, SLOTS, counts_drawn).astype(jnp.int32)


def block_levels(own_key, extent, cuts, low, high):
    def one(dim, shards_of):
        steps = jax.random.uniform(jax.random.fold_in(jax.random.fold_in(own_key, 6), dim), (shards_of,), jnp.float32, low / len(cuts), high / len(cuts))
        return jnp.repeat(jnp.exp(steps), extent[dim] // shards_of).reshape((-1,) + (1,) * (len(extent) - dim - 1))

    loudness = one(*cuts[0])
    for cut in cuts[1:]:
        loudness = loudness * one(*cut)
    return loudness


def normal_values(own_key, dims, deviation, bound, shards=(), kind=jnp.bfloat16):
    entries = jax.random.normal(own_key, dims, jnp.float32) * deviation
    if len(shards) > 0:
        entries = block_levels(own_key, dims, shards, -0.22, 0.18) * entries
    return jnp.clip(entries, min=-bound, max=bound).astype(kind)


def setup_inputs(seed: int = 0) -> dict:
    key_list = jax.random.split(jax.random.key(seed), 4)
    activations = normal_values(key_list[0], (CLIENTS, SLOTS, HH, IMG_W, CH), 1.0, 6.0, ((0, 4), (2, 8)))
    sample_count = draw_sample_count(jax.random.fold_in(key_list[3], 71), 0)
    client_weights = normal_values(key_list[2], (CLIENTS, KK, COUT), 1.0, 6.0, ((0, 4), (1, 8)))
    return {"activations": activations, "sample_count": sample_count, "client_weights": client_weights}


keep_off = 0.9


def patch_rows(images):
    groups, slots, img_height, img_width, channel_count = images.shape
    padded = jnp.pad(images, [(0, 0), (0, 0), (1, 1), (1, 1), (0, 0)])
    shifted = [padded[:, :, row_off:row_off + img_height, col_off:col_off + img_width, :] for row_off in range(3) for col_off in range(3)]
    stacked = jnp.stack(shifted, axis=-1)
    return stacked.reshape(groups, slots * img_height * img_width, channel_count * 9)


def reference(activations, sample_count, client_weights):
    live = lax.broadcasted_iota(jnp.int32, (CLIENTS, SLOTS), 1) < sample_count[:, None]
    masked = jnp.where(live[:, :, None, None, None], activations, jnp.zeros_like(activations))
    patches = patch_rows(masked)
    scales = 1.0 / (CLIENTS * sample_count.astype(jnp.float32) * (HH * IMG_W))

    def accumulate(running, inputs):
        patch_one, scale_one, weight_one = inputs
        gram_part = jnp.dot(patch_one.T, patch_one, preferred_element_type=jnp.float32)
        outputs = jnp.dot(patch_one, weight_one, preferred_element_type=jnp.float32).astype(jnp.bfloat16)
        cross = jnp.dot(patch_one.T, outputs, preferred_element_type=jnp.float32)
        diag_part = jnp.sum(jnp.square(patch_one.astype(jnp.float32)), axis=0)
        rhs_part = keep_off * cross + (1.0 - keep_off) * diag_part[:, None] * weight_one.astype(jnp.float32)
        return (running[0] + scale_one * gram_part, running[1] + scale_one * rhs_part), None

    start_state = (jnp.zeros((KK, KK), jnp.float32), jnp.zeros((KK, COUT), jnp.float32))
    (summed, merged_rhs), _ = lax.scan(accumulate, start_state, (patches, scales, client_weights))
    on_diag = lax.broadcasted_iota(jnp.int32, (KK, KK), 0) == lax.broadcasted_iota(jnp.int32, (KK, KK), 1)
    merged_gram = jnp.where(on_diag, summed, keep_off * summed)
    return merged_gram, merged_rhs
```

```python
import functools

import jax
import jax.numpy as jnp
from jax import lax
from jax.experimental import pallas as pl
from jax.experimental.pallas import tpu as pltpu
from jax.sharding import PartitionSpec as P

keep_off = 0.9
LANES = 128


def expand(x_ref, scratch, height, width):
    channels, pixels = x_ref.shape
    lane = lax.broadcasted_iota(jnp.int32, (1, pixels), 1)
    col = lane % width
    row = (lane // width) % height

    def shifted(value, step, inside):
        return jnp.where(inside, pltpu.roll(value, (-step) % pixels, 1), 0.0)

    for first in range(0, channels, 16):
        size = min(16, channels - first)
        base = x_ref[first : first + size, :].astype(jnp.float32)
        for b in range(3):
            if b == 1:
                across = base
            else:
                across = shifted(base, b - 1, (col + (b - 1) >= 0) & (col + (b - 1) < width))
            for a in range(3):
                if a == 1:
                    both = across
                else:
                    both = shifted(across, (a - 1) * width, (row + (a - 1) >= 0) & (row + (a - 1) < height))
                for chunk in range(pixels // LANES):
                    scratch[chunk, pl.ds(first * 9 + 3 * a + b, size, stride=9), :] = both[
                        :, chunk * LANES : (chunk + 1) * LANES
                    ]


def gram_kernel(height, width, first_ref, x_ref, own_ref, scale_ref, gram_ref, mine_ref, wide, narrow, mine_wide):
    step = pl.program_id(0)
    chunks = wide.shape[0]

    @pl.when(step == 0)
    def _():
        expand(own_ref, mine_wide, height, width)
        for chunk in range(chunks):
            part = slice(chunk * LANES, (chunk + 1) * LANES)
            mine_ref[:, part] = (mine_wide[chunk] * scale_ref[:, part]).astype(jnp.bfloat16)

    expand(x_ref, wide, height, width)
    for chunk in range(chunks):
        narrow[:, chunk * LANES : (chunk + 1) * LANES] = wide[chunk].astype(jnp.bfloat16)
    product = lax.dot_general(
        mine_ref[...], narrow[...], (((1,), (1,)), ((), ())), preferred_element_type=jnp.float32
    )
    where_diag = first_ref[0] - step * product.shape[1]
    on_diag = (
        lax.broadcasted_iota(jnp.int32, product.shape, 1)
        == lax.broadcasted_iota(jnp.int32, product.shape, 0) + where_diag
    )
    gram_ref[...] = jnp.where(on_diag, product, keep_off * product)


def gram_call(first_row, xt, own, scale_row, height, width):
    channels, pixels = xt.shape
    mine = own.shape[0]
    tile = LANES
    return pl.pallas_call(
        functools.partial(gram_kernel, height, width),
        grid=(channels // tile,),
        in_specs=[
            pl.BlockSpec(memory_space=pltpu.SMEM),
            pl.BlockSpec((tile, pixels), lambda j: (j, 0)),
            pl.BlockSpec((mine, pixels), lambda j: (0, 0)),
            pl.BlockSpec((1, pixels), lambda j: (0, 0)),
        ],
        out_specs=[
            pl.BlockSpec((mine * 9, tile * 9), lambda j: (0, j)),
            pl.BlockSpec((mine * 9, pixels), lambda j: (0, 0)),
        ],
        out_shape=[
            jax.ShapeDtypeStruct((mine * 9, channels * 9), jnp.float32),
            jax.ShapeDtypeStruct((mine * 9, pixels), jnp.bfloat16),
        ],
        scratch_shapes=[
            pltpu.VMEM((pixels // LANES, tile * 9, LANES), jnp.float32),
            pltpu.VMEM((tile * 9, pixels), jnp.bfloat16),
            pltpu.VMEM((pixels // LANES, mine * 9, LANES), jnp.float32),
        ],
        compiler_params=pltpu.CompilerParams(vmem_limit_bytes=60 * 1024 * 1024),
        cost_estimate=pl.CostEstimate(
            flops=2 * mine * 9 * channels * 9 * pixels,
            bytes_accessed=mine * channels * 81 * 4,
            transcendentals=0,
        ),
    )(first_row, xt, own, scale_row)


def local_kernel(height, width, x_ref, scale_ref, w_ref, out_ref, damp_ref, wide):
    group = pl.program_id(1)
    expand(x_ref.at[0], wide, height, width)
    weights = w_ref[0]
    square = jnp.zeros((wide.shape[1], 1), jnp.float32)
    for chunk in range(wide.shape[0]):
        patch = wide[chunk]
        square += jnp.sum(patch * patch, axis=1, keepdims=True)
        out_ref[0, chunk * LANES : (chunk + 1) * LANES, :] = lax.dot_general(
            patch.astype(jnp.bfloat16), weights, (((0,), (0,)), ((), ())), preferred_element_type=jnp.float32
        )
    term = (square * (scale_ref[group] * (1.0 - keep_off))) * weights.astype(jnp.float32)

    @pl.when(group == 0)
    def _():
        damp_ref[...] = term

    @pl.when(group > 0)
    def _():
        damp_ref[...] += term


def local_call(x_own, my_scale, weights, height, width):
    groups, channels, pixels = x_own.shape
    rows, columns = weights.shape[1:]
    half = columns // 2
    return pl.pallas_call(
        functools.partial(local_kernel, height, width),
        grid=(2, groups),
        in_specs=[
            pl.BlockSpec((1, channels, pixels), lambda n, i: (i, 0, 0)),
            pl.BlockSpec(memory_space=pltpu.SMEM),
            pl.BlockSpec((1, rows, half), lambda n, i: (i, 0, n)),
        ],
        out_specs=[
            pl.BlockSpec((1, pixels, half), lambda n, i: (i, 0, n)),
            pl.BlockSpec((rows, half), lambda n, i: (0, n)),
        ],
        out_shape=[
            jax.ShapeDtypeStruct((groups, pixels, columns), jnp.float32),
            jax.ShapeDtypeStruct((rows, columns), jnp.float32),
        ],
        scratch_shapes=[pltpu.VMEM((pixels // LANES, rows, LANES), jnp.float32)],
        compiler_params=pltpu.CompilerParams(vmem_limit_bytes=60 * 1024 * 1024),
        cost_estimate=pl.CostEstimate(
            flops=2 * groups * pixels * rows * columns,
            bytes_accessed=groups * rows * columns * 2,
            transcendentals=0,
        ),
    )(x_own, my_scale, weights)


def body(activations, sample_count, client_weights):
    blk_count = lax.axis_size("blk")
    client_here = lax.axis_index("client")
    blk_here = lax.axis_index("blk")
    group_size, slot_count, rows_here, width, channels = activations.shape
    height = rows_here * blk_count
    client_total = sample_count.shape[0]
    client_groups = client_total // group_size
    image = slot_count * height * width
    scale = 1.0 / (client_total * sample_count.astype(jnp.float32) * (height * width))
    live = lax.broadcasted_iota(jnp.int32, (client_total, slot_count), 1) < sample_count[:, None]

    gathered = lax.all_gather(activations, ("client", "blk"), axis=0, tiled=False)
    gathered = gathered.reshape(
        client_groups, blk_count, group_size, slot_count, rows_here, width, channels
    )
    xt = gathered.transpose(6, 0, 2, 3, 1, 4, 5).reshape(channels, client_total, slot_count, height * width)
    xt = jnp.where(live[None, :, :, None], xt, jnp.zeros_like(xt)).reshape(channels, client_total * image)

    tile = channels // blk_count
    mine = tile // client_groups
    tile_x = lax.dynamic_slice_in_dim(xt, blk_here * tile, tile, 0)
    own_x = lax.dynamic_slice_in_dim(tile_x, client_here * mine, mine, 0)
    group_x = lax.dynamic_slice_in_dim(tile_x, client_here * group_size * image, group_size * image, 1)
    group_x = group_x.reshape(tile, group_size, image).transpose(1, 0, 2)
    my_scale = lax.dynamic_slice_in_dim(scale, client_here * group_size, group_size)

    partial_out, damp = local_call(group_x, my_scale, client_weights, height, width)
    partial_out = partial_out.reshape(group_size * image, -1)
    out_share = lax.psum_scatter(partial_out, "blk", scatter_dimension=0, tiled=True)
    outs = lax.all_gather(out_share.astype(jnp.bfloat16), ("client", "blk"), axis=0, tiled=True)
    damp_mine = lax.psum_scatter(damp.astype(jnp.bfloat16), "client", scatter_dimension=0, tiled=True)

    first_row = (blk_here * tile + client_here * mine) * 9
    scale_row = jnp.repeat(scale, image)[None, :]
    gram, scaled = gram_call(
        first_row.astype(jnp.int32)[None], xt, own_x, scale_row, height, width
    )
    cross = jnp.dot(scaled, outs, preferred_element_type=jnp.float32)
    return gram, keep_off * cross + damp_mine.astype(jnp.float32)


def solution(mesh):
    in_specs = (P("client", None, "blk", None, None), P(), P("client", "blk", None))
    out_specs = (P(("blk", "client"), None), P(("blk", "client"), None))
    return jax.shard_map(body, mesh=mesh, in_specs=in_specs, out_specs=out_specs, check_vma=False)
```

```python
import functools

import jax
import jax.numpy as jnp
from jax import lax
from jax.experimental import pallas as pl
from jax.experimental.pallas import tpu as pltpu
from jax.sharding import PartitionSpec as P

keep_off = 0.9
LANES = 128


MESH = pl.DeviceIdType.MESH


def expand(base_of, live, channels, scratch, height, stride, width):
    pixels = live.shape[1]
    lane = lax.broadcasted_iota(jnp.int32, (1, pixels), 1)
    col = lane % width
    row = (lane // stride) % height

    def shifted(value, step, inside):
        return jnp.where(inside, pltpu.roll(value, (-step) % pixels, 1), 0.0)

    for first in range(0, channels, 16):
        size = min(16, channels - first)
        base = jnp.where(live > 0.0, base_of(first, size), 0.0)
        for b in range(3):
            if b == 1:
                across = base
            else:
                across = shifted(base, b - 1, (col + (b - 1) >= 0) & (col + (b - 1) < width))
            for a in range(3):
                if a == 1:
                    both = across
                else:
                    both = shifted(across, (a - 1) * stride, (row + (a - 1) >= 0) & (row + (a - 1) < height))
                for chunk in range(pixels // LANES):
                    scratch[chunk, pl.ds(first * 9 + 3 * a + b, size, stride=9), :] = both[
                        :, chunk * LANES : (chunk + 1) * LANES
                    ]


def gather_kernel(x_ref, out_ref, recv_sem, send_sem):
    clients, blks = out_ref.shape[:2]
    rows = out_ref.shape[2]
    depth = blks // 2
    client, blk = lax.axis_index("client"), lax.axis_index("blk")
    core_mate = client + 1 - 2 * (client % 2)
    x_mate = (client + 2) % clients
    z, y = blk // 2, blk % 2
    y_mate = blk + 1 - 2 * y
    core_dev, x_dev, y_dev = (core_mate, blk), (x_mate, blk), (client, y_mate)
    up_dev, down_dev = (client, blk + 2), (client, blk - 2)
    half = rows // 2

    barrier = pltpu.get_barrier_semaphore()
    for device in (core_dev, x_dev, y_dev):
        pl.semaphore_signal(barrier, inc=1, device_id=device, device_id_type=MESH)

    @pl.when(z + 1 < depth)
    def _():
        pl.semaphore_signal(barrier, inc=1, device_id=up_dev, device_id_type=MESH)

    @pl.when(z > 0)
    def _():
        pl.semaphore_signal(barrier, inc=1, device_id=down_dev, device_id_type=MESH)

    pl.semaphore_wait(barrier, 3 + jnp.where(z > 0, 1, 0) + jnp.where(z + 1 < depth, 1, 0))

    def copy(lane, c, b, device, part=None, own=False):
        where = (c, b) if part is None else (c, b, pl.ds(part * half, half))
        dst = out_ref.at[where]
        src = dst
        if own:
            src = x_ref
        if part is None:
            recv = recv_sem.at[0, c * blks + b]
        else:
            recv = recv_sem.at[part, c * blks + b]
        return pltpu.make_async_remote_copy(
            src_ref=src,
            dst_ref=dst,
            send_sem=send_sem.at[lane, c * blks + b],
            recv_sem=recv,
            device_id=device,
            device_id_type=MESH,
        )

    def along_z(offset):
        if offset == 0:
            return None
        level = z + offset
        return (level >= 0) & (level < depth)

    def guarded(offset, action):
        inside = along_z(offset)
        if inside is None:
            action(blk)
        else:
            pl.when(inside)(lambda: action(blk + 2 * offset))

    order = [0]
    for distance in range(1, depth):
        order += [-distance, distance]

    for offset in order:

        def first(b):
            own = offset == 0
            if not own:
                copy(0, client, b, core_dev).wait_recv()
            if offset <= 0:

                @pl.when(z + 1 < depth)
                def _():
                    copy(0, client, b, up_dev, own=own).start()

            if offset >= 0:

                @pl.when(z > 0)
                def _():
                    copy(1, client, b, down_dev, own=own).start()

            copy(2, client, b, x_dev, own=own).start()
            copy(3, client, b, y_dev, own=own).start()
            copy(4, client, b, core_dev, own=own).start()

        guarded(offset, first)

    def mate_of(b):
        return b + 1 - 2 * y

    for offset in order:

        def second(b):
            copy(0, x_mate, b, core_dev).wait_recv()
            copy(3, x_mate, b, y_dev, part=0).start()
            copy(4, x_mate, b, core_dev).start()
            copy(0, client, mate_of(b), core_dev).wait_recv()
            copy(2, client, mate_of(b), x_dev, part=1).start()
            copy(4, client, mate_of(b), core_dev).start()

        guarded(offset, second)

    for offset in order:

        def third(b):
            copy(0, x_mate, mate_of(b), core_dev, part=0).wait_recv()
            copy(0, x_mate, mate_of(b), core_dev, part=1).wait_recv()
            copy(4, x_mate, mate_of(b), core_dev).start()

        guarded(offset, third)

    for offset in order:

        def fourth(b):
            far = (core_mate + 2) % clients
            for c, bb in ((core_mate, b), (far, b), (core_mate, mate_of(b)), (far, mate_of(b))):
                copy(0, c, bb, core_dev).wait_recv()
            own = offset == 0
            if offset <= 0:

                @pl.when(z + 1 < depth)
                def _():
                    copy(0, client, b, up_dev, own=own).wait_send()

            if offset >= 0:

                @pl.when(z > 0)
                def _():
                    copy(1, client, b, down_dev, own=own).wait_send()

            copy(2, client, b, x_dev, own=own).wait_send()
            copy(3, client, b, y_dev, own=own).wait_send()
            copy(4, client, b, core_dev, own=own).wait_send()
            copy(3, x_mate, b, y_dev, part=0).wait_send()
            copy(4, x_mate, b, core_dev).wait_send()
            copy(2, client, mate_of(b), x_dev, part=1).wait_send()
            copy(4, client, mate_of(b), core_dev).wait_send()
            copy(4, x_mate, mate_of(b), core_dev).wait_send()

        guarded(offset, fourth)

    out_ref[client, blk] = x_ref[...]


def gather_call(x, clients, blks):
    return pl.pallas_call(
        gather_kernel,
        in_specs=[pl.BlockSpec(memory_space=pltpu.VMEM)],
        out_specs=pl.BlockSpec(memory_space=pltpu.VMEM),
        out_shape=jax.ShapeDtypeStruct((clients, blks) + x.shape, x.dtype),
        scratch_shapes=[
            pltpu.SemaphoreType.DMA((2, clients * blks)),
            pltpu.SemaphoreType.DMA((5, clients * blks)),
        ],
        compiler_params=pltpu.CompilerParams(
            collective_id=1, has_side_effects=True, vmem_limit_bytes=40 * 1024 * 1024
        ),
    )(x)


def reduce_kernel(part_ref, out_ref, ybuf, sums, zbuf, ys, yr, zs, zr, gs, gr, fs, fr):
    pieces, depth = part_ref.shape[:2]
    client, blk = lax.axis_index("client"), lax.axis_index("blk")
    z, y = blk // 2, blk % 2
    other = 1 - y
    y_dev = (client, blk + 1 - 2 * y)

    def level(d):
        return (z + d) % depth

    def z_dev(d):
        return (client, level(d) * 2 + y)

    barrier = pltpu.get_barrier_semaphore()
    pl.semaphore_signal(barrier, inc=1, device_id=y_dev, device_id_type=MESH)
    for d in range(1, depth):
        pl.semaphore_signal(barrier, inc=1, device_id=z_dev(d), device_id_type=MESH)
    pl.semaphore_wait(barrier, depth)

    def send(src, dst, send_sem, recv_sem, device):
        return pltpu.make_async_remote_copy(
            src_ref=src, dst_ref=dst, send_sem=send_sem, recv_sem=recv_sem, device_id=device, device_id_type=MESH
        )

    def y_copy(q):
        return send(part_ref.at[q, :, other], ybuf.at[q], ys.at[q], yr.at[q], y_dev)

    def z_copy(q, d):
        return send(sums.at[q, level(d)], zbuf.at[q, d], zs.at[q, d], zr.at[q, d], z_dev(d))

    def share(q, d, to):
        here = out_ref.at[q, level(d), y]
        return send(here, here, gs.at[q, to], gr.at[q, to], z_dev(to))

    def forward(q, d, column):
        here = out_ref.at[q, level(d), column]
        return send(here, here, fs.at[q, d], fr.at[q, level(d)], y_dev)

    for q in range(pieces):
        y_copy(q).start()

    def add_y(q):
        y_copy(q).wait_recv()
        for d in range(depth):
            sums[q, level(d)] = part_ref[q, level(d), y] + ybuf[q, level(d)]
        for d in range(1, depth):
            z_copy(q, d).start()

    def add_z(q):
        total = sums[q, z]
        for d in range(1, depth):
            z_copy(q, d).wait_recv()
            total = total + zbuf[q, d]
        out_ref[q, z, y] = total.astype(jnp.bfloat16)
        for d in range(1, depth):
            share(q, 0, d).start()
        forward(q, 0, y).start()

    def pass_on(q):
        for d in range(1, depth):
            share(q, depth - d, d).wait_recv()
            forward(q, depth - d, y).start()

    for step in range(pieces + 2):
        if step < pieces:
            add_y(step)
        if 0 <= step - 1 < pieces:
            add_z(step - 1)
        if 0 <= step - 2 < pieces:
            pass_on(step - 2)

    for q in range(pieces):
        y_copy(q).wait_send()
        for d in range(1, depth):
            z_copy(q, d).wait_send()
            share(q, 0, d).wait_send()
        for d in range(depth):
            forward(q, d, y).wait_send()
            forward(q, d, other).wait_recv()


def reduce_call(partial):
    pieces, depth, two, rows, columns = partial.shape
    sem = pltpu.SemaphoreType.DMA
    return pl.pallas_call(
        reduce_kernel,
        in_specs=[pl.BlockSpec(memory_space=pltpu.VMEM)],
        out_specs=pl.BlockSpec(memory_space=pltpu.VMEM),
        out_shape=jax.ShapeDtypeStruct(partial.shape, jnp.bfloat16),
        scratch_shapes=[
            pltpu.VMEM((pieces, depth, rows, columns), jnp.float32),
            pltpu.VMEM((pieces, depth, rows, columns), jnp.float32),
            pltpu.VMEM((pieces, depth, rows, columns), jnp.float32),
            sem((pieces,)),
            sem((pieces,)),
            sem((pieces, depth)),
            sem((pieces, depth)),
            sem((pieces, depth)),
            sem((pieces, depth)),
            sem((pieces, depth)),
            sem((pieces, depth)),
        ],
        compiler_params=pltpu.CompilerParams(
            collective_id=2, has_side_effects=True, vmem_limit_bytes=50 * 1024 * 1024
        ),
    )(partial)


def gram_kernel(height, stride, width, first_ref, x_ref, own_ref, scale_ref, live_ref, gram_ref, wide, narrow, mine_wide, mine_ref, flipped):
    step = pl.program_id(0)
    chunks = wide.shape[0]

    live = live_ref[...]

    @pl.when(step == 0)
    def _():
        expand(
            lambda first, size: own_ref[first : first + size, :].astype(jnp.float32),
            live, own_ref.shape[0], mine_wide, height, stride, width,
        )
        for chunk in range(chunks):
            part = slice(chunk * LANES, (chunk + 1) * LANES)
            mine_ref[:, part] = (mine_wide[chunk] * scale_ref[:, part]).astype(jnp.bfloat16)

    flipped[...] = x_ref[...].astype(jnp.float32).T
    expand(
        lambda first, size: flipped[first : first + size, :],
        live, flipped.shape[0], wide, height, stride, width,
    )
    for chunk in range(chunks):
        narrow[:, chunk * LANES : (chunk + 1) * LANES] = wide[chunk].astype(jnp.bfloat16)
    product = lax.dot_general(
        mine_ref[...], narrow[...], (((1,), (1,)), ((), ())), preferred_element_type=jnp.float32
    )
    where_diag = first_ref[0] - step * product.shape[1]
    on_diag = (
        lax.broadcasted_iota(jnp.int32, product.shape, 1)
        == lax.broadcasted_iota(jnp.int32, product.shape, 0) + where_diag
    )
    gram_ref[...] = jnp.where(on_diag, product, keep_off * product)


def gram_call(first_row, x, own, scale_row, live_row, height, stride, width):
    pixels, channels = x.shape
    mine = own.shape[0]
    tile = LANES
    return pl.pallas_call(
        functools.partial(gram_kernel, height, stride, width),
        grid=(channels // tile,),
        in_specs=[
            pl.BlockSpec(memory_space=pltpu.SMEM),
            pl.BlockSpec((pixels, tile), lambda j: (0, j)),
            pl.BlockSpec((mine, pixels), lambda j: (0, 0)),
            pl.BlockSpec((1, pixels), lambda j: (0, 0)),
            pl.BlockSpec((1, pixels), lambda j: (0, 0)),
        ],
        out_specs=pl.BlockSpec((mine * 9, tile * 9), lambda j: (0, j)),
        out_shape=jax.ShapeDtypeStruct((mine * 9, channels * 9), jnp.float32),
        scratch_shapes=[
            pltpu.VMEM((pixels // LANES, tile * 9, LANES), jnp.float32),
            pltpu.VMEM((tile * 9, pixels), jnp.bfloat16),
            pltpu.VMEM((pixels // LANES, mine * 9, LANES), jnp.float32),
            pltpu.VMEM((mine * 9, pixels), jnp.bfloat16),
            pltpu.VMEM((tile, pixels), jnp.float32),
        ],
        compiler_params=pltpu.CompilerParams(vmem_limit_bytes=60 * 1024 * 1024),
        cost_estimate=pl.CostEstimate(
            flops=2 * mine * 9 * channels * 9 * pixels,
            bytes_accessed=mine * channels * 81 * 4,
            transcendentals=0,
        ),
    )(first_row, x, own, scale_row, live_row)


def local_kernel(height, stride, width, x_ref, live_ref, who_ref, scale_ref, w_ref, out_ref, damp_ref, patch_ref, wide, square):
    piece = pl.program_id(0)
    groups = w_ref.shape[0]
    chunks = wide.shape[0]
    who = who_ref[...]

    @pl.when(piece == 0)
    def _():
        expand(
            lambda first, size: x_ref[first : first + size, :].astype(jnp.float32),
            live_ref[...], x_ref.shape[0], wide, height, stride, width,
        )
        for group in range(groups):
            sums = jnp.zeros((wide.shape[1], 1), jnp.float32)
            for chunk in range(chunks):
                part = slice(chunk * LANES, (chunk + 1) * LANES)
                patch = wide[chunk]
                sums += jnp.sum(jnp.where(who[:, part] == group, patch * patch, 0.0), axis=1, keepdims=True)
                patch_ref[:, part] = patch.astype(jnp.bfloat16)
            square[group] = sums * (scale_ref[group] * (1.0 - keep_off))

    patches = patch_ref[...]
    total = None
    damp = None
    for group in range(groups):
        weights = w_ref[group]
        picked = jnp.where(who == group, patches, jnp.zeros_like(patches))
        term = lax.dot_general(picked, weights, (((0,), (0,)), ((), ())), preferred_element_type=jnp.float32)
        scaled = square[group] * weights.astype(jnp.float32)
        total = term if total is None else total + term
        damp = scaled if damp is None else damp + scaled
    out_ref[0] = total
    damp_ref[0] = damp


def local_call(x, live, who, my_scale, weights, pieces, height, stride, width):
    channels, pixels = x.shape
    groups, rows, columns = weights.shape
    wide = columns // pieces
    return pl.pallas_call(
        functools.partial(local_kernel, height, stride, width),
        grid=(pieces,),
        in_specs=[
            pl.BlockSpec((channels, pixels), lambda n: (0, 0)),
            pl.BlockSpec((1, pixels), lambda n: (0, 0)),
            pl.BlockSpec((1, pixels), lambda n: (0, 0)),
            pl.BlockSpec(memory_space=pltpu.SMEM),
            pl.BlockSpec((groups, rows, wide), lambda n: (0, 0, n)),
        ],
        out_specs=[
            pl.BlockSpec((1, pixels, wide), lambda n: (n, 0, 0)),
            pl.BlockSpec((1, rows, wide), lambda n: (n, 0, 0)),
            pl.BlockSpec((rows, pixels), lambda n: (0, 0)),
        ],
        out_shape=[
            jax.ShapeDtypeStruct((pieces, pixels, wide), jnp.float32),
            jax.ShapeDtypeStruct((pieces, rows, wide), jnp.float32),
            jax.ShapeDtypeStruct((rows, pixels), jnp.bfloat16),
        ],
        scratch_shapes=[
            pltpu.VMEM((pixels // LANES, rows, LANES), jnp.float32),
            pltpu.VMEM((groups, rows, 1), jnp.float32),
        ],
        compiler_params=pltpu.CompilerParams(vmem_limit_bytes=60 * 1024 * 1024),
        cost_estimate=pl.CostEstimate(
            flops=2 * groups * pixels * rows * columns,
            bytes_accessed=groups * rows * columns * 2,
            transcendentals=0,
        ),
    )(x, live, who, my_scale, weights)


def cross_kernel(patch_ref, scale_ref, outs_ref, damp_ref, rhs_ref):
    scaled = (patch_ref[...].astype(jnp.float32) * scale_ref[...]).astype(jnp.bfloat16)
    cross = jnp.dot(scaled, outs_ref[0], preferred_element_type=jnp.float32)
    rhs_ref[...] = keep_off * cross + damp_ref[0]


def cross_call(patches, scale_row, outs, damp):
    rows, pixels = patches.shape
    pieces, _, wide = outs.shape
    return pl.pallas_call(
        cross_kernel,
        grid=(pieces,),
        in_specs=[
            pl.BlockSpec((rows, pixels), lambda n: (0, 0)),
            pl.BlockSpec((1, pixels), lambda n: (0, 0)),
            pl.BlockSpec((1, pixels, wide), lambda n: (n, 0, 0)),
            pl.BlockSpec((1, rows, wide), lambda n: (n, 0, 0)),
        ],
        out_specs=pl.BlockSpec((rows, wide), lambda n: (0, n)),
        out_shape=jax.ShapeDtypeStruct((rows, pieces * wide), jnp.float32),
        compiler_params=pltpu.CompilerParams(vmem_limit_bytes=60 * 1024 * 1024),
    )(patches, scale_row, outs, damp)


def body(activations, sample_count, client_weights):
    blk_count = lax.axis_size("blk")
    client_here = lax.axis_index("client")
    blk_here = lax.axis_index("blk")
    group_size, slot_count, rows_here, width, channels = activations.shape
    height = rows_here * blk_count
    client_total = sample_count.shape[0]
    client_groups = client_total // group_size
    stride = group_size * slot_count * width
    group_pixels = height * stride
    scale = 1.0 / (client_total * sample_count.astype(jnp.float32) * (height * width))

    shard = activations.transpose(2, 0, 1, 3, 4).reshape(rows_here * stride, channels)
    gathered = gather_call(shard, client_groups, blk_count).reshape(client_groups * group_pixels, channels)

    def per_pixel(value):
        value = value.reshape(client_groups, 1, group_size, slot_count, 1)
        full = jnp.broadcast_to(value, (client_groups, height, group_size, slot_count, width))
        return full.reshape(1, client_groups * group_pixels)

    slots = lax.broadcasted_iota(jnp.int32, (client_total, slot_count), 1)
    live = per_pixel((slots < sample_count[:, None]).astype(jnp.float32))
    scale_row = per_pixel(jnp.broadcast_to(scale[:, None], (client_total, slot_count)))
    member = lax.broadcasted_iota(jnp.int32, (client_total, slot_count), 0) % group_size
    who = per_pixel(member)[:, :group_pixels]

    tile = channels // blk_count
    mine = tile // client_groups
    first = blk_here * tile
    own = first + client_here * mine
    start = client_here * group_pixels
    own_x = lax.dynamic_slice_in_dim(gathered, own, mine, 1).T
    group_x = lax.dynamic_slice(gathered, (start, first), (group_pixels, tile)).T
    my_live = lax.dynamic_slice_in_dim(live, start, group_pixels, 1)
    my_scale_row = lax.dynamic_slice_in_dim(scale_row, start, group_pixels, 1)
    my_scale = lax.dynamic_slice_in_dim(scale, client_here * group_size, group_size)

    columns = client_weights.shape[2]
    pieces = columns // 256 if columns % 256 == 0 else 1
    partial_out, damp, patches = local_call(
        group_x, my_live, who, my_scale, client_weights, pieces, height, stride, width
    )
    wide = columns // pieces
    outs = reduce_call(partial_out.reshape(pieces, blk_count // 2, 2, group_pixels // blk_count, wide))
    rhs = cross_call(patches, my_scale_row, outs.reshape(pieces, group_pixels, wide), damp)

    core, side = client_here % 2, client_here // 2
    rhs = rhs.reshape(client_groups // 2, 2, mine * 9, columns)
    away = lax.dynamic_index_in_dim(rhs, 1 - core, 1, False).astype(jnp.bfloat16)
    keep = lax.dynamic_index_in_dim(rhs, core, 1, False)
    back = lax.ppermute(away, "client", [(c, c + 1 - 2 * (c % 2)) for c in range(client_groups)])
    keep = keep + back.astype(jnp.float32)
    away = lax.dynamic_index_in_dim(keep, 1 - side, 0, False).astype(jnp.bfloat16)
    keep = lax.dynamic_index_in_dim(keep, side, 0, False)
    back = lax.ppermute(away, "client", [(c, (c + 2) % client_groups) for c in range(client_groups)])

    gram = gram_call(
        (own * 9).astype(jnp.int32)[None], gathered, own_x, scale_row, live, height, stride, width
    )
    return gram, keep + back.astype(jnp.float32)


def solution(mesh):
    in_specs = (P("client", None, "blk", None, None), P(), P("client", "blk", None))
    out_specs = (P(("blk", "client"), None), P(("blk", "client"), None))
    return jax.shard_map(body, mesh=mesh, in_specs=in_specs, out_specs=out_specs, check_vma=False)
```

```python
import functools

import jax
import jax.numpy as jnp
from jax import lax
from jax.experimental import pallas as pl
from jax.experimental.pallas import tpu as pltpu
from jax.sharding import PartitionSpec as P

keep_off = 0.9
LANES = 128


MESH = pl.DeviceIdType.MESH


def pixel_rows(count_ref, base, pixels, groups, slots, height, stride, width):
    lane = lax.broadcasted_iota(jnp.int32, (1, pixels), 1)
    slot = (lane // width) % slots
    client = (lane // (height * stride)) * groups + (lane // (slots * width)) % groups
    count = jnp.zeros((1, pixels), jnp.int32)
    for index in range(pixels // (height * slots * width)):
        count = jnp.where(client == index, count_ref[base + index], count)
    live = jnp.where(slot < count, 1.0, 0.0)
    total = count_ref.shape[0] * height * width
    return live, 1.0 / (total * count.astype(jnp.float32))


def expand(base_of, live, channels, scratch, height, stride, width):
    pixels = live.shape[1]
    lane = lax.broadcasted_iota(jnp.int32, (1, pixels), 1)
    col = lane % width
    row = (lane // stride) % height

    def shifted(value, step, inside):
        return jnp.where(inside, pltpu.roll(value, (-step) % pixels, 1), 0.0)

    for first in range(0, channels, 16):
        size = min(16, channels - first)
        base = jnp.where(live > 0.0, base_of(first, size), 0.0)
        for b in range(3):
            if b == 1:
                across = base
            else:
                across = shifted(base, b - 1, (col + (b - 1) >= 0) & (col + (b - 1) < width))
            for a in range(3):
                if a == 1:
                    both = across
                else:
                    both = shifted(across, (a - 1) * stride, (row + (a - 1) >= 0) & (row + (a - 1) < height))
                for chunk in range(pixels // LANES):
                    scratch[chunk, pl.ds(first * 9 + 3 * a + b, size, stride=9), :] = both[
                        :, chunk * LANES : (chunk + 1) * LANES
                    ]


def gather_kernel(x_ref, out_ref, recv_sem, send_sem):
    clients, blks = out_ref.shape[:2]
    rows = out_ref.shape[2]
    depth = blks // 2
    client, blk = lax.axis_index("client"), lax.axis_index("blk")
    core_mate = client + 1 - 2 * (client % 2)
    x_mate = (client + 2) % clients
    z, y = blk // 2, blk % 2
    y_mate = blk + 1 - 2 * y
    core_dev, x_dev, y_dev = (core_mate, blk), (x_mate, blk), (client, y_mate)
    up_dev, down_dev = (client, blk + 2), (client, blk - 2)
    half = rows // 2

    barrier = pltpu.get_barrier_semaphore()
    for device in (core_dev, x_dev, y_dev):
        pl.semaphore_signal(barrier, inc=1, device_id=device, device_id_type=MESH)

    @pl.when(z + 1 < depth)
    def _():
        pl.semaphore_signal(barrier, inc=1, device_id=up_dev, device_id_type=MESH)

    @pl.when(z > 0)
    def _():
        pl.semaphore_signal(barrier, inc=1, device_id=down_dev, device_id_type=MESH)

    pl.semaphore_wait(barrier, 3 + jnp.where(z > 0, 1, 0) + jnp.where(z + 1 < depth, 1, 0))

    def copy(lane, c, b, device, part=None, own=False):
        where = (c, b) if part is None else (c, b, pl.ds(part * half, half))
        dst = out_ref.at[where]
        src = dst
        if own:
            src = x_ref
        if part is None:
            recv = recv_sem.at[0, c * blks + b]
        else:
            recv = recv_sem.at[part, c * blks + b]
        return pltpu.make_async_remote_copy(
            src_ref=src,
            dst_ref=dst,
            send_sem=send_sem.at[lane, c * blks + b],
            recv_sem=recv,
            device_id=device,
            device_id_type=MESH,
        )

    def along_z(offset):
        if offset == 0:
            return None
        level = z + offset
        return (level >= 0) & (level < depth)

    def guarded(offset, action):
        inside = along_z(offset)
        if inside is None:
            action(blk)
        else:
            pl.when(inside)(lambda: action(blk + 2 * offset))

    order = [0]
    for distance in range(1, depth):
        order += [-distance, distance]

    for offset in order:

        def first(b):
            own = offset == 0
            if not own:
                copy(0, client, b, core_dev).wait_recv()
            if offset <= 0:

                @pl.when(z + 1 < depth)
                def _():
                    copy(0, client, b, up_dev, own=own).start()

            if offset >= 0:

                @pl.when(z > 0)
                def _():
                    copy(1, client, b, down_dev, own=own).start()

            copy(2, client, b, x_dev, own=own).start()
            copy(3, client, b, y_dev, own=own).start()
            copy(4, client, b, core_dev, own=own).start()

        guarded(offset, first)

    def mate_of(b):
        return b + 1 - 2 * y

    for offset in order:

        def second(b):
            copy(0, x_mate, b, core_dev).wait_recv()
            copy(3, x_mate, b, y_dev, part=0).start()
            copy(4, x_mate, b, core_dev).start()
            copy(0, client, mate_of(b), core_dev).wait_recv()
            copy(2, client, mate_of(b), x_dev, part=1).start()
            copy(4, client, mate_of(b), core_dev).start()

        guarded(offset, second)

    for offset in order:

        def third(b):
            copy(0, x_mate, mate_of(b), core_dev, part=0).wait_recv()
            copy(0, x_mate, mate_of(b), core_dev, part=1).wait_recv()
            copy(4, x_mate, mate_of(b), core_dev).start()

        guarded(offset, third)

    for offset in order:

        def fourth(b):
            far = (core_mate + 2) % clients
            for c, bb in ((core_mate, b), (far, b), (core_mate, mate_of(b)), (far, mate_of(b))):
                copy(0, c, bb, core_dev).wait_recv()
            own = offset == 0
            if offset <= 0:

                @pl.when(z + 1 < depth)
                def _():
                    copy(0, client, b, up_dev, own=own).wait_send()

            if offset >= 0:

                @pl.when(z > 0)
                def _():
                    copy(1, client, b, down_dev, own=own).wait_send()

            copy(2, client, b, x_dev, own=own).wait_send()
            copy(3, client, b, y_dev, own=own).wait_send()
            copy(4, client, b, core_dev, own=own).wait_send()
            copy(3, x_mate, b, y_dev, part=0).wait_send()
            copy(4, x_mate, b, core_dev).wait_send()
            copy(2, client, mate_of(b), x_dev, part=1).wait_send()
            copy(4, client, mate_of(b), core_dev).wait_send()
            copy(4, x_mate, mate_of(b), core_dev).wait_send()

        guarded(offset, fourth)

    out_ref[client, blk] = x_ref[...]


def gather_call(x, clients, blks):
    return pl.pallas_call(
        gather_kernel,
        in_specs=[pl.BlockSpec(memory_space=pltpu.VMEM)],
        out_specs=pl.BlockSpec(memory_space=pltpu.VMEM),
        out_shape=jax.ShapeDtypeStruct((clients, blks) + x.shape, x.dtype),
        scratch_shapes=[
            pltpu.SemaphoreType.DMA((2, clients * blks)),
            pltpu.SemaphoreType.DMA((5, clients * blks)),
        ],
        compiler_params=pltpu.CompilerParams(
            collective_id=1, has_side_effects=True, vmem_limit_bytes=40 * 1024 * 1024
        ),
    )(x)


def rhs_kernel(
    height, stride, width, groups, slots, count_ref, x_ref, w_ref, keep_ref, away_ref,
    wbuf, wide, patch, scaled, square, part_ref, ybuf, sums, zbuf, obuf, rbuf, abuf, cbuf,
    ws, ys, yr, zs, zr, gs, gr, fs, fr, cs, cr,
):
    pieces, depth = part_ref.shape[:2]
    cols = part_ref.shape[4]
    pixels = x_ref.shape[1]
    tall = wide.shape[1]
    client, blk = lax.axis_index("client"), lax.axis_index("blk")
    z, y = blk // 2, blk % 2
    core, side = client % 2, client // 2
    other = 1 - y
    y_dev = (client, blk + 1 - 2 * y)
    core_dev = (client + 1 - 2 * core, blk)
    mine = keep_ref.shape[0]

    def level(d):
        return (z + d) % depth

    def z_dev(d):
        return (client, level(d) * 2 + y)

    def w_copy(q):
        return pltpu.make_async_copy(w_ref.at[:, :, pl.ds(q * cols, cols)], wbuf.at[q], ws.at[q])

    for q in range(pieces):
        w_copy(q).start()

    barrier = pltpu.get_barrier_semaphore()
    pl.semaphore_signal(barrier, inc=1, device_id=y_dev, device_id_type=MESH)
    pl.semaphore_signal(barrier, inc=1, device_id=core_dev, device_id_type=MESH)
    for d in range(1, depth):
        pl.semaphore_signal(barrier, inc=1, device_id=z_dev(d), device_id_type=MESH)

    live, scale = pixel_rows(count_ref, client * groups, pixels, groups, slots, height, stride, width)
    who = (lax.broadcasted_iota(jnp.int32, (1, pixels), 1) // (slots * width)) % groups
    expand(
        lambda first, size: x_ref[first : first + size, :].astype(jnp.float32),
        live, x_ref.shape[0], wide, height, stride, width,
    )
    for chunk in range(wide.shape[0]):
        span = slice(chunk * LANES, (chunk + 1) * LANES)
        value = wide[chunk]
        patch[:, span] = value.astype(jnp.bfloat16)
        scaled[:, span] = (value * scale[:, span]).astype(jnp.bfloat16)
    pl.semaphore_wait(barrier, depth + 1)

    def send(src, dst, send_sem, recv_sem, device):
        return pltpu.make_async_remote_copy(
            src_ref=src, dst_ref=dst, send_sem=send_sem, recv_sem=recv_sem, device_id=device, device_id_type=MESH
        )

    def y_copy(q):
        return send(part_ref.at[q, :, other], ybuf.at[q], ys.at[q], yr.at[q], y_dev)

    def z_copy(q, d):
        return send(sums.at[q, level(d)], zbuf.at[q, d], zs.at[q, d], zr.at[q, d], z_dev(d))

    def share(q, d, to):
        here = obuf.at[q, level(d), y]
        return send(here, here, gs.at[q, to], gr.at[q, to], z_dev(to))

    def forward(q, d, column):
        here = obuf.at[q, level(d), column]
        return send(here, here, fs.at[q, d], fr.at[q, level(d)], y_dev)

    def core_copy(q):
        return send(abuf.at[q], cbuf.at[q], cs.at[q], cr.at[q], core_dev)

    def multiply(q):
        w_copy(q).wait()
        total = None
        for group in range(groups):
            picked = jnp.where(who == group, patch[...].astype(jnp.float32), 0.0).astype(jnp.bfloat16)
            term = lax.dot_general(
                picked, wbuf[q, group], (((0,), (0,)), ((), ())), preferred_element_type=jnp.float32
            )
            total = term if total is None else total + term
        part_ref[q] = total.reshape(part_ref.shape[1:])
        y_copy(q).start()

    def damping():
        for group in range(groups):
            term = jnp.zeros((tall, 1), jnp.float32)
            for chunk in range(wide.shape[0]):
                span = slice(chunk * LANES, (chunk + 1) * LANES)
                value = wide[chunk]
                value = jnp.where(who[:, span] == group, value * value * scale[:, span], 0.0)
                term += jnp.sum(value, axis=1, keepdims=True)
            square[group] = term * (1.0 - keep_off)

    def damp(q):
        total = None
        for group in range(groups):
            term = square[group] * wbuf[q, group].astype(jnp.float32)
            total = term if total is None else total + term
        rbuf[q] = total

    def add_y(q):
        y_copy(q).wait_recv()
        for d in range(depth):
            sums[q, level(d)] = part_ref[q, level(d), y] + ybuf[q, level(d)]
        for d in range(1, depth):
            z_copy(q, d).start()

    def add_z(q):
        total = sums[q, z]
        for d in range(1, depth):
            z_copy(q, d).wait_recv()
            total = total + zbuf[q, d]
        obuf[q, z, y] = total.astype(jnp.bfloat16)
        for d in range(1, depth):
            share(q, 0, d).start()
        forward(q, 0, y).start()

    def pass_on(q):
        for d in range(1, depth):
            share(q, depth - d, d).wait_recv()
            forward(q, depth - d, y).start()

    def rows_of(q, holder):
        if mine % 8 == 0:
            return rbuf[q, pl.ds(pl.multiple_of(holder * mine, 8), mine), :]
        value = rbuf[q, :mine, :]
        for index in range(1, tall // mine):
            value = jnp.where(holder == index, rbuf[q, index * mine : (index + 1) * mine, :], value)
        return value

    def cross(q):
        for d in range(depth):
            forward(q, d, other).wait_recv()
        product = jnp.dot(scaled[...], obuf[q].reshape(pixels, cols), preferred_element_type=jnp.float32)
        rbuf[q] = rbuf[q] + keep_off * product
        for far in range(2):
            abuf[q, far] = rows_of(q, far * 2 + 1 - core).astype(jnp.bfloat16)
        core_copy(q).start()

    def finish(q):
        core_copy(q).wait_recv()
        span = slice(q * cols, (q + 1) * cols)
        keep_ref[:, span] = rows_of(q, client) + cbuf[q, side].astype(jnp.float32)
        far = 1 - side
        away = rows_of(q, far * 2 + core) + cbuf[q, far].astype(jnp.float32)
        away_ref[:, span] = away.astype(jnp.bfloat16)

    for q in range(pieces):
        multiply(q)
    damping()
    for step in range(pieces + 4):
        if step < pieces:
            add_y(step)
        if 0 <= step - 1 < pieces:
            add_z(step - 1)
        if step < pieces:
            damp(step)
        if 0 <= step - 2 < pieces:
            pass_on(step - 2)
        if 0 <= step - 3 < pieces:
            cross(step - 3)
        if 0 <= step - 4 < pieces:
            finish(step - 4)

    for q in range(pieces):
        y_copy(q).wait_send()
        core_copy(q).wait_send()
        for d in range(1, depth):
            z_copy(q, d).wait_send()
            share(q, 0, d).wait_send()
        for d in range(depth):
            forward(q, d, y).wait_send()


def rhs_call(counts, x, weights, blks, mine, slots, height, stride, width):
    channels, pixels = x.shape
    groups, tall, columns = weights.shape
    pieces = columns // 256 if columns % 256 == 0 else 1
    cols = columns // pieces
    depth = blks // 2
    rows = pixels // blks
    sem = pltpu.SemaphoreType.DMA
    hop = pltpu.VMEM((pieces, depth, rows, cols), jnp.float32)
    return pl.pallas_call(
        functools.partial(rhs_kernel, height, stride, width, groups, slots),
        in_specs=[
            pl.BlockSpec(memory_space=pltpu.SMEM),
            pl.BlockSpec(memory_space=pltpu.VMEM),
            pl.BlockSpec(memory_space=pl.ANY),
        ],
        out_specs=[pl.BlockSpec(memory_space=pltpu.VMEM)] * 2,
        out_shape=[
            jax.ShapeDtypeStruct((mine, columns), jnp.float32),
            jax.ShapeDtypeStruct((mine, columns), jnp.bfloat16),
        ],
        scratch_shapes=[
            pltpu.VMEM((pieces, groups, tall, cols), jnp.bfloat16),
            pltpu.VMEM((pixels // LANES, tall, LANES), jnp.float32),
            pltpu.VMEM((tall, pixels), jnp.bfloat16),
            pltpu.VMEM((tall, pixels), jnp.bfloat16),
            pltpu.VMEM((groups, tall, 1), jnp.float32),
            pltpu.VMEM((pieces, depth, 2, rows, cols), jnp.float32),
            hop,
            hop,
            hop,
            pltpu.VMEM((pieces, depth, 2, rows, cols), jnp.bfloat16),
            pltpu.VMEM((pieces, tall, cols), jnp.float32),
            pltpu.VMEM((pieces, 2, mine, cols), jnp.bfloat16),
            pltpu.VMEM((pieces, 2, mine, cols), jnp.bfloat16),
            sem((pieces,)),
            sem((pieces,)),
            sem((pieces,)),
        ]
        + [sem((pieces, depth))] * 6
        + [sem((pieces,))] * 2,
        compiler_params=pltpu.CompilerParams(
            collective_id=2, has_side_effects=True, vmem_limit_bytes=60 * 1024 * 1024
        ),
    )(counts, x, weights)


def gram_kernel(height, stride, width, groups, slots, first_ref, count_ref, x_ref, own_ref, gram_ref, wide, narrow, mine_wide, mine_ref, flipped):
    step = pl.program_id(0)
    chunks = wide.shape[0]

    live, scale = pixel_rows(count_ref, 0, x_ref.shape[0], groups, slots, height, stride, width)

    @pl.when(step == 0)
    def _():
        expand(
            lambda first, size: own_ref[first : first + size, :].astype(jnp.float32),
            live, own_ref.shape[0], mine_wide, height, stride, width,
        )
        for chunk in range(chunks):
            part = slice(chunk * LANES, (chunk + 1) * LANES)
            mine_ref[:, part] = (mine_wide[chunk] * scale[:, part]).astype(jnp.bfloat16)

    flipped[...] = x_ref[...].astype(jnp.float32).T
    expand(
        lambda first, size: flipped[first : first + size, :],
        live, flipped.shape[0], wide, height, stride, width,
    )
    for chunk in range(chunks):
        narrow[:, chunk * LANES : (chunk + 1) * LANES] = wide[chunk].astype(jnp.bfloat16)
    product = lax.dot_general(
        mine_ref[...], narrow[...], (((1,), (1,)), ((), ())), preferred_element_type=jnp.float32
    )
    where_diag = first_ref[0] - step * product.shape[1]
    on_diag = (
        lax.broadcasted_iota(jnp.int32, product.shape, 1)
        == lax.broadcasted_iota(jnp.int32, product.shape, 0) + where_diag
    )
    gram_ref[...] = jnp.where(on_diag, product, keep_off * product)


def gram_call(first_row, counts, x, own, groups, slots, height, stride, width):
    pixels, channels = x.shape
    mine = own.shape[0]
    tile = LANES
    return pl.pallas_call(
        functools.partial(gram_kernel, height, stride, width, groups, slots),
        grid=(channels // tile,),
        in_specs=[
            pl.BlockSpec(memory_space=pltpu.SMEM),
            pl.BlockSpec(memory_space=pltpu.SMEM),
            pl.BlockSpec((pixels, tile), lambda j: (0, j)),
            pl.BlockSpec((mine, pixels), lambda j: (0, 0)),
        ],
        out_specs=pl.BlockSpec((mine * 9, tile * 9), lambda j: (0, j)),
        out_shape=jax.ShapeDtypeStruct((mine * 9, channels * 9), jnp.float32),
        scratch_shapes=[
            pltpu.VMEM((pixels // LANES, tile * 9, LANES), jnp.float32),
            pltpu.VMEM((tile * 9, pixels), jnp.bfloat16),
            pltpu.VMEM((pixels // LANES, mine * 9, LANES), jnp.float32),
            pltpu.VMEM((mine * 9, pixels), jnp.bfloat16),
            pltpu.VMEM((tile, pixels), jnp.float32),
        ],
        compiler_params=pltpu.CompilerParams(vmem_limit_bytes=60 * 1024 * 1024),
        cost_estimate=pl.CostEstimate(
            flops=2 * mine * 9 * channels * 9 * pixels,
            bytes_accessed=mine * channels * 81 * 4,
            transcendentals=0,
        ),
    )(first_row, counts, x, own)


def body(activations, sample_count, client_weights):
    blk_count = lax.axis_size("blk")
    client_here = lax.axis_index("client")
    blk_here = lax.axis_index("blk")
    group_size, slot_count, rows_here, width, channels = activations.shape
    height = rows_here * blk_count
    client_groups = sample_count.shape[0] // group_size
    stride = group_size * slot_count * width
    group_pixels = height * stride

    shard = activations.transpose(2, 0, 1, 3, 4).reshape(rows_here * stride, channels)
    gathered = gather_call(shard, client_groups, blk_count).reshape(client_groups * group_pixels, channels)

    tile = channels // blk_count
    mine = tile // client_groups
    first = blk_here * tile
    own = first + client_here * mine
    own_x = lax.dynamic_slice_in_dim(gathered, own, mine, 1).T
    group_x = lax.dynamic_slice(gathered, (client_here * group_pixels, first), (group_pixels, tile)).T
    keep, away = rhs_call(
        sample_count, group_x, client_weights, blk_count, mine * 9, slot_count, height, stride, width
    )
    back = lax.ppermute(away, "client", [(c, (c + 2) % client_groups) for c in range(client_groups)])
    gram = gram_call(
        (own * 9).astype(jnp.int32)[None], sample_count, gathered, own_x,
        group_size, slot_count, height, stride, width,
    )
    return gram, keep + back.astype(jnp.float32)


def solution(mesh):
    in_specs = (P("client", None, "blk", None, None), P(), P("client", "blk", None))
    out_specs = (P(("blk", "client"), None), P(("blk", "client"), None))
    return jax.shard_map(body, mesh=mesh, in_specs=in_specs, out_specs=out_specs, check_vma=False)
```

```python
import functools

import jax
import jax.numpy as jnp
from jax import lax
from jax.experimental import pallas as pl
from jax.experimental.pallas import tpu as pltpu
from jax.sharding import PartitionSpec as P

keep_off = 0.9
LANES = 128


MESH = pl.DeviceIdType.MESH


def pixel_rows(count_ref, base, pixels, groups, slots, height, stride, width):
    lane = lax.broadcasted_iota(jnp.int32, (1, pixels), 1)
    slot = (lane // width) % slots
    client = (lane // (height * stride)) * groups + (lane // (slots * width)) % groups
    count = jnp.zeros((1, pixels), jnp.int32)
    for index in range(pixels // (height * slots * width)):
        count = jnp.where(client == index, count_ref[base + index], count)
    live = jnp.where(slot < count, 1.0, 0.0)
    total = count_ref.shape[0] * height * width
    return live, 1.0 / (total * count.astype(jnp.float32))


def expand(base_of, live, channels, scratch, height, stride, width):
    pixels = live.shape[1]
    lane = lax.broadcasted_iota(jnp.int32, (1, pixels), 1)
    col = lane % width
    row = (lane // stride) % height

    def shifted(value, step, inside):
        return jnp.where(inside, pltpu.roll(value, (-step) % pixels, 1), 0.0)

    for first in range(0, channels, 16):
        size = min(16, channels - first)
        base = jnp.where(live > 0.0, base_of(first, size), 0.0)
        for b in range(3):
            if b == 1:
                across = base
            else:
                across = shifted(base, b - 1, (col + (b - 1) >= 0) & (col + (b - 1) < width))
            for a in range(3):
                if a == 1:
                    both = across
                else:
                    both = shifted(across, (a - 1) * stride, (row + (a - 1) >= 0) & (row + (a - 1) < height))
                for chunk in range(pixels // LANES):
                    scratch[chunk, pl.ds(first * 9 + 3 * a + b, size, stride=9), :] = both[
                        :, chunk * LANES : (chunk + 1) * LANES
                    ]


def gather_kernel(x_ref, out_ref, recv_sem, send_sem):
    clients, blks = out_ref.shape[:2]
    rows = out_ref.shape[2]
    depth = blks // 2
    client, blk = lax.axis_index("client"), lax.axis_index("blk")
    core_mate = client + 1 - 2 * (client % 2)
    x_mate = (client + 2) % clients
    z, y = blk // 2, blk % 2
    y_mate = blk + 1 - 2 * y
    core_dev, x_dev, y_dev = (core_mate, blk), (x_mate, blk), (client, y_mate)
    up_dev, down_dev = (client, blk + 2), (client, blk - 2)
    half = rows // 2

    barrier = pltpu.get_barrier_semaphore()
    for device in (core_dev, x_dev, y_dev):
        pl.semaphore_signal(barrier, inc=1, device_id=device, device_id_type=MESH)

    @pl.when(z + 1 < depth)
    def _():
        pl.semaphore_signal(barrier, inc=1, device_id=up_dev, device_id_type=MESH)

    @pl.when(z > 0)
    def _():
        pl.semaphore_signal(barrier, inc=1, device_id=down_dev, device_id_type=MESH)

    pl.semaphore_wait(barrier, 3 + jnp.where(z > 0, 1, 0) + jnp.where(z + 1 < depth, 1, 0))

    def copy(lane, c, b, device, part=None, own=False):
        where = (c, b) if part is None else (c, b, pl.ds(part * half, half))
        dst = out_ref.at[where]
        src = dst
        if own:
            src = x_ref
        if part is None:
            recv = recv_sem.at[0, c * blks + b]
        else:
            recv = recv_sem.at[part, c * blks + b]
        return pltpu.make_async_remote_copy(
            src_ref=src,
            dst_ref=dst,
            send_sem=send_sem.at[lane, c * blks + b],
            recv_sem=recv,
            device_id=device,
            device_id_type=MESH,
        )

    def along_z(offset):
        if offset == 0:
            return None
        level = z + offset
        return (level >= 0) & (level < depth)

    def guarded(offset, action):
        inside = along_z(offset)
        if inside is None:
            action(blk)
        else:
            pl.when(inside)(lambda: action(blk + 2 * offset))

    order = [0]
    for distance in range(1, depth):
        order += [-distance, distance]

    for offset in order:

        def first(b):
            own = offset == 0
            if not own:
                copy(0, client, b, core_dev).wait_recv()
            if offset <= 0:

                @pl.when(z + 1 < depth)
                def _():
                    copy(0, client, b, up_dev, own=own).start()

            if offset >= 0:

                @pl.when(z > 0)
                def _():
                    copy(1, client, b, down_dev, own=own).start()

            copy(2, client, b, x_dev, own=own).start()
            copy(3, client, b, y_dev, own=own).start()
            copy(4, client, b, core_dev, own=own).start()

        guarded(offset, first)

    def mate_of(b):
        return b + 1 - 2 * y

    for offset in order:

        def second(b):
            copy(0, x_mate, b, core_dev).wait_recv()
            copy(3, x_mate, b, y_dev, part=0).start()
            copy(4, x_mate, b, core_dev).start()
            copy(0, client, mate_of(b), core_dev).wait_recv()
            copy(2, client, mate_of(b), x_dev, part=1).start()
            copy(4, client, mate_of(b), core_dev).start()

        guarded(offset, second)

    for offset in order:

        def third(b):
            copy(0, x_mate, mate_of(b), core_dev, part=0).wait_recv()
            copy(0, x_mate, mate_of(b), core_dev, part=1).wait_recv()
            copy(4, x_mate, mate_of(b), core_dev).start()

        guarded(offset, third)

    for offset in order:

        def fourth(b):
            far = (core_mate + 2) % clients
            for c, bb in ((core_mate, b), (far, b), (core_mate, mate_of(b)), (far, mate_of(b))):
                copy(0, c, bb, core_dev).wait_recv()
            own = offset == 0
            if offset <= 0:

                @pl.when(z + 1 < depth)
                def _():
                    copy(0, client, b, up_dev, own=own).wait_send()

            if offset >= 0:

                @pl.when(z > 0)
                def _():
                    copy(1, client, b, down_dev, own=own).wait_send()

            copy(2, client, b, x_dev, own=own).wait_send()
            copy(3, client, b, y_dev, own=own).wait_send()
            copy(4, client, b, core_dev, own=own).wait_send()
            copy(3, x_mate, b, y_dev, part=0).wait_send()
            copy(4, x_mate, b, core_dev).wait_send()
            copy(2, client, mate_of(b), x_dev, part=1).wait_send()
            copy(4, client, mate_of(b), core_dev).wait_send()
            copy(4, x_mate, mate_of(b), core_dev).wait_send()

        guarded(offset, fourth)

    out_ref[client, blk] = x_ref[...]


def gather_call(x, clients, blks):
    return pl.pallas_call(
        gather_kernel,
        in_specs=[pl.BlockSpec(memory_space=pltpu.VMEM)],
        out_specs=pl.BlockSpec(memory_space=pltpu.VMEM),
        out_shape=jax.ShapeDtypeStruct((clients, blks) + x.shape, x.dtype),
        scratch_shapes=[
            pltpu.SemaphoreType.DMA((2, clients * blks)),
            pltpu.SemaphoreType.DMA((5, clients * blks)),
        ],
        compiler_params=pltpu.CompilerParams(
            collective_id=1, has_side_effects=True, vmem_limit_bytes=40 * 1024 * 1024
        ),
    )(x)


def rhs_kernel(
    height, stride, width, groups, slots, count_ref, x_ref, w_ref, keep_ref, away_ref,
    wbuf, wide, patch, scaled, square, part_ref, ybuf, sums, zbuf, obuf, rbuf, abuf, cbuf,
    ws, ys, yr, zs, zr, gs, gr, fs, fr, cs, cr,
):
    pieces, depth = part_ref.shape[:2]
    cols = part_ref.shape[4]
    pixels = x_ref.shape[1]
    tall = wide.shape[1]
    client, blk = lax.axis_index("client"), lax.axis_index("blk")
    z, y = blk // 2, blk % 2
    core, side = client % 2, client // 2
    other = 1 - y
    y_dev = (client, blk + 1 - 2 * y)
    core_dev = (client + 1 - 2 * core, blk)
    mine = keep_ref.shape[0]

    def level(d):
        return (z + d) % depth

    def z_dev(d):
        return (client, level(d) * 2 + y)

    def w_copy(q):
        return pltpu.make_async_copy(w_ref.at[:, :, pl.ds(q * cols, cols)], wbuf.at[q], ws.at[q])

    for q in range(pieces):
        w_copy(q).start()

    barrier = pltpu.get_barrier_semaphore()
    pl.semaphore_signal(barrier, inc=1, device_id=y_dev, device_id_type=MESH)
    pl.semaphore_signal(barrier, inc=1, device_id=core_dev, device_id_type=MESH)
    for d in range(1, depth):
        pl.semaphore_signal(barrier, inc=1, device_id=z_dev(d), device_id_type=MESH)

    live, scale = pixel_rows(count_ref, client * groups, pixels, groups, slots, height, stride, width)
    who = (lax.broadcasted_iota(jnp.int32, (1, pixels), 1) // (slots * width)) % groups
    expand(
        lambda first, size: x_ref[first : first + size, :].astype(jnp.float32),
        live, x_ref.shape[0], wide, height, stride, width,
    )
    for chunk in range(wide.shape[0]):
        span = slice(chunk * LANES, (chunk + 1) * LANES)
        value = wide[chunk]
        patch[:, span] = value.astype(jnp.bfloat16)
        scaled[:, span] = (value * scale[:, span]).astype(jnp.bfloat16)
    pl.semaphore_wait(barrier, depth + 1)

    def send(src, dst, send_sem, recv_sem, device):
        return pltpu.make_async_remote_copy(
            src_ref=src, dst_ref=dst, send_sem=send_sem, recv_sem=recv_sem, device_id=device, device_id_type=MESH
        )

    def y_copy(q):
        return send(part_ref.at[q, :, other], ybuf.at[q], ys.at[q], yr.at[q], y_dev)

    def z_copy(q, d):
        return send(sums.at[q, level(d)], zbuf.at[q, d], zs.at[q, d], zr.at[q, d], z_dev(d))

    def share(q, d, to):
        here = obuf.at[q, level(d), y]
        return send(here, here, gs.at[q, to], gr.at[q, to], z_dev(to))

    def forward(q, d, column):
        here = obuf.at[q, level(d), column]
        return send(here, here, fs.at[q, d], fr.at[q, level(d)], y_dev)

    def core_copy(q):
        return send(abuf.at[q], cbuf.at[q], cs.at[q], cr.at[q], core_dev)

    def multiply(q):
        w_copy(q).wait()
        total = None
        for group in range(groups):
            picked = jnp.where(who == group, patch[...].astype(jnp.float32), 0.0).astype(jnp.bfloat16)
            term = lax.dot_general(
                picked, wbuf[q, group], (((0,), (0,)), ((), ())), preferred_element_type=jnp.float32
            )
            total = term if total is None else total + term
        part_ref[q] = total.reshape(part_ref.shape[1:])
        y_copy(q).start()

    def damping():
        for group in range(groups):
            term = jnp.zeros((tall, 1), jnp.float32)
            for chunk in range(wide.shape[0]):
                span = slice(chunk * LANES, (chunk + 1) * LANES)
                value = wide[chunk]
                value = jnp.where(who[:, span] == group, value * value * scale[:, span], 0.0)
                term += jnp.sum(value, axis=1, keepdims=True)
            square[group] = term * (1.0 - keep_off)

    def damp(q):
        total = None
        for group in range(groups):
            term = square[group] * wbuf[q, group].astype(jnp.float32)
            total = term if total is None else total + term
        rbuf[q] = total

    def add_y(q):
        y_copy(q).wait_recv()
        for d in range(depth):
            sums[q, level(d)] = part_ref[q, level(d), y] + ybuf[q, level(d)]
        for d in range(1, depth):
            z_copy(q, d).start()

    def add_z(q):
        total = sums[q, z]
        for d in range(1, depth):
            z_copy(q, d).wait_recv()
            total = total + zbuf[q, d]
        obuf[q, z, y] = total.astype(jnp.bfloat16)
        for d in range(1, depth):
            share(q, 0, d).start()
        forward(q, 0, y).start()

    def pass_on(q):
        for d in range(1, depth):
            share(q, depth - d, d).wait_recv()
            forward(q, depth - d, y).start()

    def rows_of(q, holder):
        if mine % 8 == 0:
            return rbuf[q, pl.ds(pl.multiple_of(holder * mine, 8), mine), :]
        value = rbuf[q, :mine, :]
        for index in range(1, tall // mine):
            value = jnp.where(holder == index, rbuf[q, index * mine : (index + 1) * mine, :], value)
        return value

    def cross(q):
        for d in range(depth):
            forward(q, d, other).wait_recv()
        product = jnp.dot(scaled[...], obuf[q].reshape(pixels, cols), preferred_element_type=jnp.float32)
        rbuf[q] = rbuf[q] + keep_off * product
        for far in range(2):
            abuf[q, far] = rows_of(q, far * 2 + 1 - core).astype(jnp.bfloat16)
        core_copy(q).start()

    def finish(q):
        core_copy(q).wait_recv()
        span = slice(q * cols, (q + 1) * cols)
        keep_ref[:, span] = rows_of(q, client) + cbuf[q, side].astype(jnp.float32)
        far = 1 - side
        away = rows_of(q, far * 2 + core) + cbuf[q, far].astype(jnp.float32)
        away_ref[:, span] = away.astype(jnp.bfloat16)

    for q in range(pieces):
        multiply(q)
    damping()
    for step in range(pieces + 4):
        if step < pieces:
            add_y(step)
        if 0 <= step - 1 < pieces:
            add_z(step - 1)
        if step < pieces:
            damp(step)
        if 0 <= step - 2 < pieces:
            pass_on(step - 2)
        if 0 <= step - 3 < pieces:
            cross(step - 3)
        if 0 <= step - 4 < pieces:
            finish(step - 4)

    for q in range(pieces):
        y_copy(q).wait_send()
        core_copy(q).wait_send()
        for d in range(1, depth):
            z_copy(q, d).wait_send()
            share(q, 0, d).wait_send()
        for d in range(depth):
            forward(q, d, y).wait_send()


def rhs_call(counts, x, weights, blks, mine, slots, height, stride, width):
    channels, pixels = x.shape
    groups, tall, columns = weights.shape
    pieces = columns // 256 if columns % 256 == 0 else 1
    cols = columns // pieces
    depth = blks // 2
    rows = pixels // blks
    sem = pltpu.SemaphoreType.DMA
    hop = pltpu.VMEM((pieces, depth, rows, cols), jnp.float32)
    return pl.pallas_call(
        functools.partial(rhs_kernel, height, stride, width, groups, slots),
        in_specs=[
            pl.BlockSpec(memory_space=pltpu.SMEM),
            pl.BlockSpec(memory_space=pltpu.VMEM),
            pl.BlockSpec(memory_space=pl.ANY),
        ],
        out_specs=[pl.BlockSpec(memory_space=pltpu.VMEM)] * 2,
        out_shape=[
            jax.ShapeDtypeStruct((mine, columns), jnp.float32),
            jax.ShapeDtypeStruct((mine, columns), jnp.bfloat16),
        ],
        scratch_shapes=[
            pltpu.VMEM((pieces, groups, tall, cols), jnp.bfloat16),
            pltpu.VMEM((pixels // LANES, tall, LANES), jnp.float32),
            pltpu.VMEM((tall, pixels), jnp.bfloat16),
            pltpu.VMEM((tall, pixels), jnp.bfloat16),
            pltpu.VMEM((groups, tall, 1), jnp.float32),
            pltpu.VMEM((pieces, depth, 2, rows, cols), jnp.float32),
            hop,
            hop,
            hop,
            pltpu.VMEM((pieces, depth, 2, rows, cols), jnp.bfloat16),
            pltpu.VMEM((pieces, tall, cols), jnp.float32),
            pltpu.VMEM((pieces, 2, mine, cols), jnp.bfloat16),
            pltpu.VMEM((pieces, 2, mine, cols), jnp.bfloat16),
            sem((pieces,)),
            sem((pieces,)),
            sem((pieces,)),
        ]
        + [sem((pieces, depth))] * 6
        + [sem((pieces,))] * 2,
        compiler_params=pltpu.CompilerParams(
            collective_id=2, has_side_effects=True, vmem_limit_bytes=60 * 1024 * 1024
        ),
    )(counts, x, weights)


def gram_kernel(height, stride, width, groups, slots, first_ref, count_ref, x_ref, own_ref, gram_ref, wide, narrow, mine_wide, mine_ref, flipped):
    step = pl.program_id(0)
    chunks = wide.shape[0]

    live, scale = pixel_rows(count_ref, 0, x_ref.shape[0], groups, slots, height, stride, width)

    @pl.when(step == 0)
    def _():
        expand(
            lambda first, size: own_ref[first : first + size, :].astype(jnp.float32),
            live, own_ref.shape[0], mine_wide, height, stride, width,
        )
        for chunk in range(chunks):
            part = slice(chunk * LANES, (chunk + 1) * LANES)
            mine_ref[:, part] = (mine_wide[chunk] * scale[:, part]).astype(jnp.bfloat16)

    product = lax.dot_general(
        mine_ref[...], narrow[...], (((1,), (1,)), ((), ())), preferred_element_type=jnp.float32
    )
    where_diag = first_ref[0] - (step - 1) * product.shape[1]
    on_diag = (
        lax.broadcasted_iota(jnp.int32, product.shape, 1)
        == lax.broadcasted_iota(jnp.int32, product.shape, 0) + where_diag
    )
    gram_ref[...] = jnp.where(on_diag, product, keep_off * product)
    flipped[...] = x_ref[...].astype(jnp.float32).T
    expand(
        lambda first, size: flipped[first : first + size, :],
        live, flipped.shape[0], wide, height, stride, width,
    )
    for chunk in range(chunks):
        narrow[:, chunk * LANES : (chunk + 1) * LANES] = wide[chunk].astype(jnp.bfloat16)


def gram_call(first_row, counts, x, own, groups, slots, height, stride, width):
    pixels, channels = x.shape
    mine = own.shape[0]
    tile = LANES
    return pl.pallas_call(
        functools.partial(gram_kernel, height, stride, width, groups, slots),
        grid=(channels // tile + 1,),
        in_specs=[
            pl.BlockSpec(memory_space=pltpu.SMEM),
            pl.BlockSpec(memory_space=pltpu.SMEM),
            pl.BlockSpec((pixels, tile), lambda j: (0, jnp.minimum(j, channels // tile - 1))),
            pl.BlockSpec((mine, pixels), lambda j: (0, 0)),
        ],
        out_specs=pl.BlockSpec((mine * 9, tile * 9), lambda j: (0, jnp.maximum(j - 1, 0))),
        out_shape=jax.ShapeDtypeStruct((mine * 9, channels * 9), jnp.float32),
        scratch_shapes=[
            pltpu.VMEM((pixels // LANES, tile * 9, LANES), jnp.float32),
            pltpu.VMEM((tile * 9, pixels), jnp.bfloat16),
            pltpu.VMEM((pixels // LANES, mine * 9, LANES), jnp.float32),
            pltpu.VMEM((mine * 9, pixels), jnp.bfloat16),
            pltpu.VMEM((tile, pixels), jnp.float32),
        ],
        compiler_params=pltpu.CompilerParams(vmem_limit_bytes=60 * 1024 * 1024),
        cost_estimate=pl.CostEstimate(
            flops=2 * mine * 9 * channels * 9 * pixels,
            bytes_accessed=mine * channels * 81 * 4,
            transcendentals=0,
        ),
    )(first_row, counts, x, own)


def body(activations, sample_count, client_weights):
    blk_count = lax.axis_size("blk")
    client_here = lax.axis_index("client")
    blk_here = lax.axis_index("blk")
    group_size, slot_count, rows_here, width, channels = activations.shape
    height = rows_here * blk_count
    client_groups = sample_count.shape[0] // group_size
    stride = group_size * slot_count * width
    group_pixels = height * stride

    shard = activations.transpose(2, 0, 1, 3, 4).reshape(rows_here * stride, channels)
    gathered = gather_call(shard, client_groups, blk_count).reshape(client_groups * group_pixels, channels)

    tile = channels // blk_count
    mine = tile // client_groups
    first = blk_here * tile
    own = first + client_here * mine
    own_x = lax.dynamic_slice_in_dim(gathered, own, mine, 1).T
    group_x = lax.dynamic_slice(gathered, (client_here * group_pixels, first), (group_pixels, tile)).T
    keep, away = rhs_call(
        sample_count, group_x, client_weights, blk_count, mine * 9, slot_count, height, stride, width
    )
    back = lax.ppermute(away, "client", [(c, (c + 2) % client_groups) for c in range(client_groups)])
    gram = gram_call(
        (own * 9).astype(jnp.int32)[None], sample_count, gathered, own_x,
        group_size, slot_count, height, stride, width,
    )
    return gram, keep + back.astype(jnp.float32)


def solution(mesh):
    in_specs = (P("client", None, "blk", None, None), P(), P("client", "blk", None))
    out_specs = (P(("blk", "client"), None), P(("blk", "client"), None))
    return jax.shard_map(body, mesh=mesh, in_specs=in_specs, out_specs=out_specs, check_vma=False)
```
